32 devices in a mesh: group: 4 (over y, x), owner: 8 (over z, core).
Axes of the slice: x: 2, y: 2, z: 4, core: 2. Of those that a mesh axis runs over, the one named last changes fastest.
Arguments:
- field: float32 [64, 4096], P(None, ('group', 'owner')), may hold values from -6 to 6
- contrast: float32 [64, 4096], P(None, ('group', 'owner')), may hold values from 0.1 to 2
- incident: float32 [64, 4096], P(None, ('group', 'owner')), may hold values from -6 to 6
- near_lists: int32 [27, 4096], P(None, ('group', 'owner')), may hold values from -1 to 128, as said below
- far_lists: int32 [316, 4672], P(None, ('group', 'owner')), may hold values from -1 to 128, as said below
- near_mats: float32 [27, 64, 64], replicated, may hold values from -0.15625 to 0.15625
- far_mats: float32 [316, 49, 49], replicated, may hold values from -0.0625 to 0.0625
- up_mats: float32 [8, 49, 49], replicated, may hold values from -0.3125 to 0.3125
- down_mats: float32 [8, 49, 49], replicated, may hold values from -0.875 to 0.875
- moment_map: float32 [49, 64], replicated, may hold values from -0.75 to 0.75
- local_map: float32 [64, 49], replicated, may hold values from -0.5 to 0.5
Outputs:
- new_field: float32 [64, 4096], P(None, ('group', 'owner'))
The draws below stay inside these ranges and needn't reach their ends.
Inputs may be any that keep to these rules, and one draw needn't show every extreme that they name: -1 marks an empty slot; otherwise b + near_lists[k, b] - 64 is a leaf box, and slot 13 of every box holds 64. `far_lists`: -1 marks an empty slot; otherwise the entry names a box of the column's level as the steps say: below level 2 an entry of 0 to w_l, at level 2 any box of that level.
All inputs are finite; a program needn't handle non-finite values.
Results may differ from the reference program's by a relative error of at most 0.0003.
Values sent between devices are 32-bit elements; how exact they have to be, the bound alone decides.
No kernel may reach another device: no remote copies, remote signals or barrier semaphores. Data moves between devices by JAX's collectives and lax.ppermute only.
A program may use at most 128 MiB of HBM per device.

```python
import math
import jax
import jax.numpy as jnp
import numpy as np
from jax import lax

CELLS = 64
TERMS = 49
NNEAR = 27
NFAR = 316
LOCAL = 2
TOPS = 2
BPD = 128
NEARW = 64
BOXDEV = 146
NBOX = 4096
FARCOLS = 4672
N_GROUP = 4
N_OWNER = 8


def draw_near_lists(key, part):
    key_shift, key_keep, key_load = jax.random.split(key, 3)
    devices = NBOX // BPD
    slots = jnp.arange(NNEAR, dtype=jnp.int32)[:, None]
    boxes = jnp.arange(NBOX, dtype=jnp.int32)[None, :]
    offset = jax.random.randint(key_shift, (NNEAR, NBOX), -NEARW, NEARW + 1)
    burden = jax.random.randint(key_load, (devices,), 2, 8)
    ceiling = jnp.repeat(burden, BPD)[None, :]
    kept = jax.random.randint(key_keep, (NNEAR, NBOX), 0, 8) < ceiling
    centre = slots == NNEAR // 2
    reach_top = (slots == 1) & (boxes == 0)
    offset = jnp.where(reach_top, NEARW, offset)
    kept = (kept | centre | reach_top) & jnp.logical_not((slots == 0) & (boxes == 0))
    partner = jnp.clip(boxes + jnp.where(centre, 0, offset), 0, NBOX - 1)
    value = partner - boxes + NEARW
    return jnp.where(kept, value, -1).astype(jnp.int32)


def draw_far_lists(key, part):
    spans = [TOPS * 8 ** (LOCAL - level) for level in range(LOCAL + 1)]
    devices = NBOX // BPD
    level_of = np.concatenate([np.full(span, level) for level, span in enumerate(spans)])
    inside = np.concatenate([np.arange(span) for span in spans])
    span_of = np.concatenate([np.full(span, span) for span in spans])
    device_of = np.repeat(np.arange(devices), BOXDEV)
    span_every = np.tile(span_of, devices)
    level_every = jnp.asarray(np.tile(level_of, devices), jnp.int32)[None, :]
    own_box = jnp.asarray(device_of * span_every + np.tile(inside, devices), jnp.int32)[None, :]
    level_count = jnp.asarray(span_every * devices, jnp.int32)[None, :]
    half_wide = jnp.asarray(span_every // 2, jnp.int32)[None, :]
    key_pick, key_keep, key_load = jax.random.split(key, 3)
    drawn = jax.random.randint(key_pick, (NFAR, FARCOLS), 0, 1 << 20)
    offset = drawn % (2 * half_wide + 1) - half_wide
    slots = jnp.arange(NFAR, dtype=jnp.int32)[:, None]
    columns = jnp.arange(FARCOLS, dtype=jnp.int32)[None, :]
    reach_close = (slots == 1) & (columns == 0)
    offset = jnp.where(reach_close, half_wide, offset)
    close_value = jnp.clip(own_box + offset, 0, level_count - 1) - own_box + half_wide
    top_value = drawn % level_count
    reach_top = (slots == 2) & (columns == BOXDEV - 1)
    top_value = jnp.where(reach_top, level_count - 1, top_value)
    value = jnp.where(level_every == LOCAL, top_value, close_value)
    burden = jax.random.randint(key_load, (devices,), 2, 8)
    ceiling = jnp.repeat(burden, BOXDEV)[None, :]
    kept = jax.random.randint(key_keep, (NFAR, FARCOLS), 0, 8) < ceiling
    kept = (kept | reach_close | reach_top) & jnp.logical_not((slots == 0) & (columns == 0))
    return jnp.where(kept, value, -1).astype(jnp.int32)


def steps_of(own_key, dims, cuts, smallest, high):
    level = 1.0
    for axis_at, parts in cuts:
        steps = jax.random.uniform(jax.random.fold_in(jax.random.fold_in(own_key, 6), axis_at), (parts,), jnp.float32, smallest / len(cuts), high / len(cuts))
        level = level * jnp.repeat(jnp.exp(steps), dims[axis_at] // parts).reshape((-1,) + (1,) * (len(dims) - 1 - axis_at))
    return level


def gaussian(stream_key, extent, deviation, most, cuts=(), kind=jnp.bfloat16):
    factor_of = steps_of(stream_key, extent, cuts, -0.22, 0.18) if cuts else 1.0
    values = jax.random.normal(stream_key, extent, jnp.float32) * deviation * factor_of
    return jnp.minimum(jnp.maximum(values, -most), most).astype(kind)


def setup_inputs(seed: int = 0) -> dict:
    key_of = jax.random.split(jax.random.key(seed), 12)
    field = gaussian(key_of[0], (CELLS, NBOX), 1.0, 6.0, ((1, 32),), jnp.float32)
    contrast = jnp.clip(jnp.exp(math.log(2.0) - 2.9957323 * jax.random.uniform(key_of[1], (CELLS, NBOX), jnp.float32) ** steps_of(key_of[1], (CELLS, NBOX), ((1, 32),), -0.2, 0.2)), 0.1, 2.0)
    incident = gaussian(key_of[2], (CELLS, NBOX), 1.0, 6.0, ((1, 32),), jnp.float32)
    near_lists = draw_near_lists(jax.random.fold_in(key_of[11], 71), 0)
    far_lists = draw_far_lists(jax.random.fold_in(key_of[11], 71), 0)
    near_mats = gaussian(key_of[5], (NNEAR, CELLS, CELLS), (CELLS * NNEAR) ** -0.5, 0.15625, (), jnp.float32)
    far_mats = gaussian(key_of[6], (NFAR, TERMS, TERMS), (TERMS * NFAR // 2) ** -0.5, 0.0625, (), jnp.float32)
    up_mats = gaussian(key_of[7], (8, TERMS, TERMS), (8 * TERMS) ** -0.5, 0.3125, (), jnp.float32)
    down_mats = gaussian(key_of[8], (8, TERMS, TERMS), TERMS ** -0.5, 0.875, (), jnp.float32)
    moment_map = gaussian(key_of[9], (TERMS, CELLS), CELLS ** -0.5, 0.75, (), jnp.float32)
    local_map = gaussian(key_of[10], (CELLS, TERMS), (TERMS * (LOCAL + 1)) ** -0.5, 0.5, (), jnp.float32)
    return {"field": field, "contrast": contrast, "incident": incident, "near_lists": near_lists, "far_lists": far_lists, "near_mats": near_mats, "far_mats": far_mats, "up_mats": up_mats, "down_mats": down_mats, "moment_map": moment_map, "local_map": local_map}


HIGHEST_PRECISION = lax.Precision.HIGHEST


def upward(moments, up_mats):
    children = moments.reshape(moments.shape[0], -1, 8)
    return jnp.einsum("cst,tjc->sj", up_mats, children, precision=HIGHEST_PRECISION)


def downward(parents, down_mats):
    children = jnp.einsum("cst,tj->sjc", down_mats, parents, precision=HIGHEST_PRECISION)
    return children.reshape(parents.shape[0], -1)


def slot_sum(values, lists, mats):
    def add_slot(total, inputs):
        slot_row, matrix = inputs
        valid = slot_row >= 0
        picked = jnp.where(valid[None, :], values[:, jnp.where(valid, slot_row, 0)], 0.0)
        return total + jnp.dot(matrix, picked, precision=HIGHEST_PRECISION), None

    start_total = jnp.zeros((mats.shape[1], lists.shape[1]), jnp.float32)
    total, _ = lax.scan(add_slot, start_total, (lists, mats))
    return total


def reference(field, contrast, incident, near_lists, far_lists, near_mats, far_mats, up_mats, down_mats, moment_map, local_map):
    devices = N_GROUP * N_OWNER
    source = contrast * field
    leaf_ids = jnp.arange(NBOX, dtype=jnp.int32)[None, :]
    near_boxes = jnp.where(near_lists >= 0, leaf_ids + near_lists - NEARW, -1).astype(jnp.int32)
    near_field = slot_sum(source, near_boxes, near_mats)
    moments = [jnp.dot(moment_map, source, precision=HIGHEST_PRECISION)]
    for level in range(LOCAL):
        moments.append(upward(moments[-1], up_mats))
    spans = [TOPS * 8 ** (LOCAL - level) for level in range(LOCAL + 1)]
    offsets = [sum(spans[:level]) for level in range(LOCAL + 1)]
    table = far_lists.reshape(NFAR, devices, BOXDEV)
    expansion = None
    for level in range(LOCAL, -1, -1):
        level_lists = table[:, :, offsets[level]:offsets[level] + spans[level]].reshape(NFAR, spans[level] * devices)
        if level < LOCAL:
            own_ids = jnp.arange(spans[level] * devices, dtype=jnp.int32)[None, :]
            level_lists = jnp.where(level_lists >= 0, own_ids + level_lists - spans[level] // 2, -1).astype(jnp.int32)
        far_term = slot_sum(moments[level], level_lists, far_mats)
        if level == LOCAL:
            expansion = far_term
        else:
            expansion = far_term + downward(expansion, down_mats)
    far_field = jnp.dot(local_map, expansion, precision=HIGHEST_PRECISION)
    return incident + near_field + far_field
```

```python
import jax
import jax.numpy as jnp
from jax import lax
from jax.experimental import pallas as pl
from jax.experimental.pallas import tpu as pltpu
from jax.sharding import PartitionSpec as P

AXES = ("group", "owner")
HIGH = lax.Precision.HIGHEST
LANES = 128
GROUP = 7
VMEM = pl.BlockSpec(memory_space=pltpu.VMEM)
SMEM = pl.BlockSpec(memory_space=pltpu.SMEM)
NN = (((1,), (0,)), ((), ()))
NT = (((1,), (1,)), ((), ()))
GATHER = lax.GatherDimensionNumbers(
    offset_dims=(),
    collapsed_slice_dims=(1,),
    start_index_map=(1,),
    operand_batching_dims=(0,),
    start_indices_batching_dims=(0,),
)


def lane_gather(values, lanes):
    return lax.gather(
        values,
        lanes[..., None],
        GATHER,
        (1, 1),
        mode=lax.GatherScatterMode.PROMISE_IN_BOUNDS,
    )


def exact_dot(lhs, rhs, dims):
    return lax.dot_general(
        lhs, rhs, dims, precision=HIGH, preferred_element_type=jnp.float32
    )


def fast_dot(lhs, rhs, dims):
    return lax.dot_general(lhs, rhs, dims, preferred_element_type=jnp.float32)


def halves(value):
    upper = value.astype(jnp.bfloat16)
    lower = (value - upper.astype(jnp.float32)).astype(jnp.bfloat16)
    return upper, lower


def split_dot(lhs, rhs, dims):
    (lhs_hi, lhs_lo), (rhs_hi, rhs_lo) = lhs, rhs
    return (
        fast_dot(lhs_hi, rhs_hi, dims)
        + fast_dot(lhs_hi, rhs_lo, dims)
        + fast_dot(lhs_lo, rhs_hi, dims)
    )


def parents_of(children_ref, count, up_ref):
    terms = up_ref.shape[1]
    total = None
    for c in range(8):
        part = exact_dot(
            children_ref[pl.ds(c, count, stride=8), :],
            up_ref[pl.ds(c, terms, stride=8), :],
            NT,
        )
        total = part if total is None else total + part
    return total


def source_kernel(field_ref, contrast_ref, map_ref, up_ref, source_ref, tops_ref, low, mid):
    source = contrast_ref[...] * field_ref[...]
    source_ref[...] = source
    terms = map_ref.shape[0]
    low[...] = exact_dot(map_ref[...], source, NN).T
    mid[...] = parents_of(low, mid.shape[0], up_ref)
    tops = parents_of(mid, mid.shape[0] // 8, up_ref)
    devices = tops_ref.shape[0]
    tops_ref[...] = jnp.zeros(tops_ref.shape, jnp.float32)
    tops_ref[:, 0:terms] = jnp.broadcast_to(tops[0:1], (devices, terms))
    tops_ref[:, 64 : 64 + terms] = jnp.broadcast_to(tops[1:2], (devices, terms))


def local_kernel(
    source_ref,
    first_ref,
    second_ref,
    incident_ref,
    near_lists_ref,
    far_lists_ref,
    near_mats_ref,
    far_mats_ref,
    map_ref,
    up_ref,
    odd_ref,
    partial_ref,
    far_ref,
    rim,
    low_own,
    low_rim,
    low_rows,
    mid,
    mid_lanes,
    lane_at,
    kind_at,
    picked_hi,
    picked_lo,
):
    leaves = source_ref.shape[1]
    half = leaves // 2
    terms = map_ref.shape[0]
    mids = leaves // 8
    slots = far_mats_ref.shape[2]
    lane = lax.broadcasted_iota(jnp.int32, source_ref.shape, 1)
    odd = odd_ref[0]
    from_first = (lane // half) == odd
    rim[...] = jnp.where(from_first, first_ref[...], second_ref[...])
    own_low = exact_dot(map_ref[...], source_ref[...], NN)
    rim_low = exact_dot(map_ref[...], rim[...], NN)
    low_own[0:terms, :] = own_low
    low_rim[0:terms, :] = rim_low
    low_rows[0:leaves, :] = own_low.T
    low_rows[leaves : 2 * leaves, :] = rim_low.T
    mid[...] = parents_of(low_rows, 2 * mids, up_ref)
    mid_lanes[...] = jnp.zeros(mid_lanes.shape, jnp.float32)
    mid_lanes[0:terms, 0 : 2 * mids] = mid[...].T

    lane_at[...] = jnp.zeros(lane_at.shape, jnp.int32)
    kind_at[...] = jnp.zeros(kind_at.shape, jnp.int32)
    entry = far_lists_ref[0:leaves, :]
    at = lax.broadcasted_iota(jnp.int32, entry.shape, 0) + entry - half
    own = (at >= 0) & (at < leaves)
    lane_at[0:leaves, 0:slots] = at & (leaves - 1)
    kind_at[0:leaves, 0:slots] = jnp.where(entry < 0, 0, jnp.where(own, 1, 2))
    entry = far_lists_ref[leaves : leaves + mids, :]
    at = lax.broadcasted_iota(jnp.int32, entry.shape, 0) + entry - mids // 2
    own = (at >= 0) & (at < mids)
    lane_at[leaves : leaves + mids, 0:slots] = (at & (mids - 1)) + jnp.where(own, 0, mids)
    kind_at[leaves : leaves + mids, 0:slots] = jnp.where(entry < 0, 0, 1)

    near_lane = lax.broadcasted_iota(jnp.int32, (8, leaves), 1)
    cells = source_ref.shape[0]

    def near_step(k, total):
        entry = jnp.broadcast_to(near_lists_ref[pl.ds(k, 1), :], (8, leaves))
        at = near_lane + entry - half
        inside = (at >= 0) & (at < leaves)
        use_own = (entry >= 0) & inside
        use_rim = (entry >= 0) & jnp.logical_not(inside)
        lanes = at & (leaves - 1)
        rows = []
        for r in range(0, cells, 8):
            from_own = lane_gather(source_ref[r : r + 8, :], lanes)
            from_rim = lane_gather(rim[r : r + 8, :], lanes)
            rows.append(
                jnp.where(use_own, from_own, jnp.where(use_rim, from_rim, 0.0))
            )
        picked = halves(jnp.concatenate(rows, axis=0))
        return total + split_dot(halves(near_mats_ref[k]), picked, NN)

    partial_ref[...] = lax.fori_loop(
        0, near_lists_ref.shape[0], near_step, incident_ref[...], unroll=3
    )

    def far_step(g, total):
        for row in range(0, leaves + mids, 16):
            for column in range(0, lane_at.shape[1], LANES):
                lanes = lane_at[row : row + 16, column : column + LANES]
                kinds = kind_at[row : row + 16, column : column + LANES]
                use_own = kinds == 1
                use_rim = kinds == 2
                for u in range(GROUP):
                    t = g * GROUP + u
                    if row < leaves:
                        own_row = jnp.broadcast_to(low_own[pl.ds(t, 1), :], (16, LANES))
                        rim_row = jnp.broadcast_to(low_rim[pl.ds(t, 1), :], (16, LANES))
                        value = jnp.where(
                            use_own,
                            lane_gather(own_row, lanes),
                            jnp.where(use_rim, lane_gather(rim_row, lanes), 0.0),
                        )
                    else:
                        mid_row = jnp.broadcast_to(mid_lanes[pl.ds(t, 1), :], (16, LANES))
                        value = jnp.where(use_own, lane_gather(mid_row, lanes), 0.0)
                    upper, lower = halves(value)
                    picked_hi[u, row : row + 16, column : column + LANES] = upper
                    picked_lo[u, row : row + 16, column : column + LANES] = lower
        for u in range(GROUP):
            t = g * GROUP + u
            matrix = halves(far_mats_ref[:, pl.ds(t, 1), :][:, 0, :])
            picked = (picked_hi[u, :, 0:slots], picked_lo[u, :, 0:slots])
            total = total + split_dot(picked, matrix, NT)
        return total

    far_ref[...] = lax.fori_loop(
        0, terms // GROUP, far_step, jnp.zeros(far_ref.shape, jnp.float32)
    )


def final_kernel(
    every_top_ref,
    far_lists_ref,
    far_mats_ref,
    far_ref,
    partial_ref,
    down_ref,
    local_ref,
    out_ref,
    top_lanes,
    sums,
    tops,
    mid,
    low,
):
    devices = every_top_ref.shape[0]
    terms = far_ref.shape[1]
    leaves = partial_ref.shape[1]
    mids = leaves // 8
    count = far_lists_ref.shape[0] - leaves - mids
    slots = far_mats_ref.shape[2]
    every = every_top_ref[...]
    both = jnp.concatenate([every[:, 0:64], every[:, 64:128]], axis=0)
    tiles = top_lanes.shape[0]
    wide = tiles * LANES
    if wide > both.shape[0]:
        both = jnp.concatenate(
            [both, jnp.zeros((wide - both.shape[0], both.shape[1]), jnp.float32)], axis=0
        )
    for tile in range(tiles):
        top_lanes[tile] = both[tile * LANES : (tile + 1) * LANES].T
    rows = top_lanes.shape[1] // 8
    picked = []
    for j in range(count):
        entry = far_lists_ref[pl.ds(leaves + mids + j, 1), :]
        code = jnp.where(entry < 0, -1, (entry & 1) * devices + (entry >> 1))
        columns = []
        for column in range(0, slots, LANES):
            width = min(LANES, slots - column)
            part = code[:, column : column + width]
            if width < LANES:
                part = jnp.concatenate(
                    [part, jnp.full((1, LANES - width), -1, jnp.int32)], axis=1
                )
            part = jnp.broadcast_to(part, (56, LANES))
            value = jnp.zeros((56, LANES), jnp.float32)
            for tile in range(tiles):
                here = (part >> 7) == tile
                value = jnp.where(
                    here, lane_gather(top_lanes[tile, 0:56, :], part & (LANES - 1)), value
                )
            columns.append(value)
        picked.append(jnp.concatenate(columns, axis=1)[0:terms, 0:slots])

    def top_step(s, carry):
        matrix = far_mats_ref[s]
        for j in range(count):
            sums[j, pl.ds(s, 1), :] = jnp.sum(matrix * picked[j], axis=0, keepdims=True)
        return carry

    lax.fori_loop(0, terms, top_step, 0, unroll=7)
    ones = jnp.ones((8, slots), jnp.float32)
    for j in range(count):
        tops[pl.ds(j, 1), :] = exact_dot(ones, sums[j], NT)[0:1]
    top_rows = tops[...]
    for c in range(8):
        matrix = down_ref[pl.ds(c, terms, stride=8), :]
        part = exact_dot(top_rows, matrix, NT)
        mid[pl.ds(c, count, stride=8), :] = part[0:count]
    mid_rows = mid[...] + far_ref[leaves : leaves + mids, :]
    for c in range(8):
        matrix = down_ref[pl.ds(c, terms, stride=8), :]
        low[pl.ds(c, mids, stride=8), :] = exact_dot(mid_rows, matrix, NT)
    low_rows = low[...] + far_ref[0:leaves, :]
    out_ref[...] = partial_ref[...] + exact_dot(local_ref[...].T, low_rows, NT)


def body(
    field,
    contrast,
    incident,
    near_lists,
    far_lists,
    near_mats,
    far_mats,
    up_mats,
    down_mats,
    moment_map,
    local_map,
):
    devices = lax.axis_size(AXES)
    rank = lax.axis_index(AXES)
    cells, leaves = field.shape
    terms = moment_map.shape[0]
    mids = leaves // 8
    slots = far_mats.shape[0]
    assert leaves == LANES and terms % GROUP == 0 and far_lists.shape[1] == 146
    up_rows = up_mats.transpose(1, 0, 2).reshape(8 * terms, terms)
    down_rows = down_mats.transpose(1, 0, 2).reshape(8 * terms, terms)
    far_cube = far_mats.transpose(1, 2, 0)
    far_rows = far_lists.T
    wide = -(-slots // LANES) * LANES
    f32 = jnp.float32

    source, own_tops = pl.pallas_call(
        source_kernel,
        out_shape=(
            jax.ShapeDtypeStruct((cells, leaves), f32),
            jax.ShapeDtypeStruct((devices, LANES), f32),
        ),
        in_specs=[VMEM] * 4,
        out_specs=(VMEM, VMEM),
        scratch_shapes=[pltpu.VMEM((leaves, terms), f32), pltpu.VMEM((mids, terms), f32)],
    )(field, contrast, moment_map, up_rows)

    pairs = [(i, i ^ 1) for i in range(devices)]
    shifted = [(0, 0), (devices - 1, devices - 1)]
    for i in range(1, devices - 1, 2):
        shifted += [(i, i + 1), (i + 1, i)]
    first = lax.ppermute(source, AXES, pairs)
    second = lax.ppermute(source, AXES, shifted)
    every_top = lax.all_to_all(own_tops, AXES, split_axis=0, concat_axis=0, tiled=True)

    odd = jnp.reshape(rank % 2, (1,)).astype(jnp.int32)
    partial, far_sums = pl.pallas_call(
        local_kernel,
        out_shape=(
            jax.ShapeDtypeStruct((cells, leaves), f32),
            jax.ShapeDtypeStruct((leaves + mids, terms), f32),
        ),
        in_specs=[VMEM] * 10 + [SMEM],
        out_specs=(VMEM, VMEM),
        scratch_shapes=[
            pltpu.VMEM((cells, leaves), f32),
            pltpu.VMEM((56, leaves), f32),
            pltpu.VMEM((56, leaves), f32),
            pltpu.VMEM((2 * leaves, terms), f32),
            pltpu.VMEM((2 * mids, terms), f32),
            pltpu.VMEM((56, LANES), f32),
            pltpu.VMEM((leaves + mids, wide), jnp.int32),
            pltpu.VMEM((leaves + mids, wide), jnp.int32),
            pltpu.VMEM((GROUP, leaves + mids, wide), jnp.bfloat16),
            pltpu.VMEM((GROUP, leaves + mids, wide), jnp.bfloat16),
        ],
        compiler_params=pltpu.CompilerParams(vmem_limit_bytes=40 << 20),
    )(
        source,
        first,
        second,
        incident,
        near_lists,
        far_rows,
        near_mats,
        far_cube,
        moment_map,
        up_rows,
        odd,
    )

    tiles = -(-2 * devices // LANES)
    return pl.pallas_call(
        final_kernel,
        out_shape=jax.ShapeDtypeStruct((cells, leaves), f32),
        in_specs=[VMEM] * 7,
        out_specs=VMEM,
        scratch_shapes=[
            pltpu.VMEM((tiles, 64, LANES), f32),
            pltpu.VMEM((2, terms, slots), f32),
            pltpu.VMEM((8, terms), f32),
            pltpu.VMEM((mids, terms), f32),
            pltpu.VMEM((leaves, terms), f32),
        ],
        compiler_params=pltpu.CompilerParams(vmem_limit_bytes=40 << 20),
    )(every_top, far_rows, far_cube, far_sums, partial, down_rows, local_map.T)


def solution(mesh):
    columns = P(None, AXES)
    in_specs = (columns,) * 5 + (P(),) * 6
    return jax.shard_map(body, mesh=mesh, in_specs=in_specs, out_specs=columns, check_vma=False)
```

```python
import jax
import jax.numpy as jnp
from jax import lax
from jax.experimental import pallas as pl
from jax.experimental.pallas import tpu as pltpu
from jax.sharding import PartitionSpec as P

AXES = ("group", "owner")
HIGH = lax.Precision.HIGHEST
LANES = 128
GROUP = 8
VMEM = pl.BlockSpec(memory_space=pltpu.VMEM)
SMEM = pl.BlockSpec(memory_space=pltpu.SMEM)
HBM = pl.BlockSpec(memory_space=pltpu.HBM)
NN = (((1,), (0,)), ((), ()))
NT = (((1,), (1,)), ((), ()))
GATHER = lax.GatherDimensionNumbers(
    offset_dims=(),
    collapsed_slice_dims=(1,),
    start_index_map=(1,),
    operand_batching_dims=(0,),
    start_indices_batching_dims=(0,),
)


def lane_gather(values, lanes):
    return lax.gather(
        values,
        lanes[..., None],
        GATHER,
        (1, 1),
        mode=lax.GatherScatterMode.PROMISE_IN_BOUNDS,
    )


def exact_dot(lhs, rhs, dims):
    return lax.dot_general(
        lhs, rhs, dims, precision=HIGH, preferred_element_type=jnp.float32
    )


def fast_dot(lhs, rhs, dims):
    return lax.dot_general(lhs, rhs, dims, preferred_element_type=jnp.float32)


def halves(value):
    upper = value.astype(jnp.bfloat16)
    lower = (value - upper.astype(jnp.float32)).astype(jnp.bfloat16)
    return upper, lower


def split_dot(lhs, rhs, dims):
    (lhs_hi, lhs_lo), (rhs_hi, rhs_lo) = lhs, rhs
    return (
        fast_dot(lhs_hi, rhs_hi, dims)
        + fast_dot(lhs_hi, rhs_lo, dims)
        + fast_dot(lhs_lo, rhs_hi, dims)
    )


def parents_of(children_ref, count, up_ref):
    terms = up_ref.shape[1]
    total = None
    for c in range(8):
        part = exact_dot(
            children_ref[pl.ds(c, count, stride=8), :],
            up_ref[pl.ds(c, terms, stride=8), :],
            NT,
        )
        total = part if total is None else total + part
    return total


def source_kernel(field_ref, contrast_ref, map_ref, up_ref, source_ref, tops_ref, low, mid):
    source = contrast_ref[...] * field_ref[...]
    source_ref[...] = source
    terms = map_ref.shape[0]
    low[...] = exact_dot(map_ref[...], source, NN).T
    mid[...] = parents_of(low, mid.shape[0], up_ref)
    tops = parents_of(mid, mid.shape[0] // 8, up_ref)
    devices = tops_ref.shape[0]
    tops_ref[...] = jnp.zeros(tops_ref.shape, jnp.float32)
    tops_ref[:, 0:terms] = jnp.broadcast_to(tops[0:1], (devices, terms))
    tops_ref[:, 64 : 64 + terms] = jnp.broadcast_to(tops[1:2], (devices, terms))


def split_block(value):
    upper, lower = halves(value)
    return jnp.concatenate([upper, lower], axis=0)


def local_kernel(
    odd_ref,
    source_hbm,
    first_hbm,
    second_hbm,
    incident_hbm,
    near_lists_hbm,
    far_lists_hbm,
    near_mats_hbm,
    far_mats_hbm,
    map_hbm,
    up_hbm,
    partial_ref,
    far_ref,
    source_ref,
    first_ref,
    second_ref,
    incident,
    near_lists,
    far_lists,
    near_mats,
    far_mats,
    map_mat,
    up_mat,
    rim,
    low_own,
    low_rim,
    low_rows,
    mid,
    mid_lanes,
    lane_at,
    kind_at,
    picked_hi,
    picked_lo,
    matrices,
    spread,
    sems,
):
    moves = [
        pltpu.make_async_copy(src, dst, sems.at[i])
        for i, (src, dst) in enumerate(
            [
                (map_hbm, map_mat),
                (source_hbm, source_ref),
                (first_hbm, first_ref),
                (second_hbm, second_ref),
                (up_hbm, up_mat),
                (far_lists_hbm, far_lists),
                (near_lists_hbm, near_lists),
                (near_mats_hbm, near_mats),
                (incident_hbm, incident),
                (far_mats_hbm, far_mats),
            ]
        )
    ]
    for move in moves:
        move.start()
    cells, leaves = source_ref.shape
    half = leaves // 2
    terms = map_mat.shape[0]
    mids = leaves // 8
    targets = leaves + mids
    slots = far_mats.shape[2]
    wide = lane_at.shape[1]
    lane_at[...] = jnp.zeros(lane_at.shape, jnp.int16)
    kind_at[...] = jnp.zeros(kind_at.shape, jnp.int16)
    mid_lanes[...] = jnp.zeros(mid_lanes.shape, jnp.float32)
    lane = lax.broadcasted_iota(jnp.int32, source_ref.shape, 1)
    from_first = (lane // half) == odd_ref[0]
    for move in moves[0:4]:
        move.wait()
    rim[...] = jnp.where(from_first, first_ref[...], second_ref[...])

    own_low = exact_dot(map_mat[...], source_ref[...], NN)
    rim_low = exact_dot(map_mat[...], rim[...], NN)
    low_own[0:terms, :] = own_low
    low_rim[0:terms, :] = rim_low
    low_rows[0:leaves, :] = own_low.T
    low_rows[leaves : 2 * leaves, :] = rim_low.T
    moves[4].wait()
    mid[...] = parents_of(low_rows, 2 * mids, up_mat)
    mid_lanes[0:terms, 0 : 2 * mids] = mid[...].T

    moves[5].wait()
    entry = far_lists[0:leaves, :]
    at = lax.broadcasted_iota(jnp.int32, entry.shape, 0) + entry - half
    own = (at >= 0) & (at < leaves)
    lane_at[0:leaves, 0:slots] = (at & (leaves - 1)).astype(jnp.int16)
    kind_at[0:leaves, 0:slots] = jnp.where(entry < 0, 0, jnp.where(own, 1, 2)).astype(jnp.int16)
    entry = far_lists[leaves:targets, :]
    at = lax.broadcasted_iota(jnp.int32, entry.shape, 0) + entry - mids // 2
    own = (at >= 0) & (at < mids)
    lanes = (at & (mids - 1)) + jnp.where(own, 0, mids)
    lane_at[leaves:targets, 0:slots] = lanes.astype(jnp.int16)
    kind_at[leaves:targets, 0:slots] = jnp.where(entry < 0, 0, 1).astype(jnp.int16)

    for move in moves[6:9]:
        move.wait()
    near_lane = lax.broadcasted_iota(jnp.int32, (8, leaves), 1)

    def near_step(k, total):
        entry = jnp.broadcast_to(near_lists[pl.ds(k, 1), :], (8, leaves))
        at = near_lane + entry - half
        inside = (at >= 0) & (at < leaves)
        use_own = (entry >= 0) & inside
        use_rim = (entry >= 0) & jnp.logical_not(inside)
        lanes = at & (leaves - 1)
        rows = []
        for r in range(0, cells, 8):
            from_own = lane_gather(source_ref[r : r + 8, :], lanes)
            from_rim = lane_gather(rim[r : r + 8, :], lanes)
            rows.append(
                jnp.where(use_own, from_own, jnp.where(use_rim, from_rim, 0.0))
            )
        picked = halves(jnp.concatenate(rows, axis=0))
        return total + split_dot(halves(near_mats[k]), picked, NN)

    partial_ref[...] = lax.fori_loop(
        0, near_lists.shape[0], near_step, incident[...], unroll=9
    )

    moves[9].wait()
    padding = jnp.zeros((terms, wide - slots), jnp.float32)
    rest = jnp.zeros((64 - terms, wide), jnp.float32)

    def far_block(first, count, cube, total):
        for u in range(count):
            for i, table in enumerate((low_own, low_rim, mid_lanes)):
                row = jnp.broadcast_to(table[pl.ds(first + u, 1), :], (16, LANES))
                spread[6 * u + 2 * i], spread[6 * u + 2 * i + 1] = halves(row)
            matrix = jnp.concatenate([cube[u], padding], axis=1)
            matrix = jnp.concatenate([matrix, rest], axis=0)
            upper, lower = halves(matrix)
            matrices[0:64, u * wide : (u + 1) * wide] = upper
            matrices[64:128, u * wide : (u + 1) * wide] = lower
        nothing = jnp.zeros((16, LANES), jnp.bfloat16)
        for row in range(0, targets, 16):
            for column in range(0, wide, LANES):
                lanes = lane_at[row : row + 16, column : column + LANES]
                kinds = kind_at[row : row + 16, column : column + LANES]
                use_own = kinds == 1
                use_rim = kinds == 2
                for u in range(count):
                    place = u * wide + column
                    for i, picked in enumerate((picked_hi, picked_lo)):
                        if row < leaves:
                            value = jnp.where(
                                use_own,
                                lane_gather(spread[6 * u + i], lanes),
                                jnp.where(
                                    use_rim, lane_gather(spread[6 * u + 2 + i], lanes), nothing
                                ),
                            )
                        else:
                            value = jnp.where(
                                use_own, lane_gather(spread[6 * u + 4 + i], lanes), nothing
                            )
                        picked[row : row + 16, place : place + LANES] = value
        depth = count * wide
        both = fast_dot(picked_hi[:, 0:depth], matrices[:, 0:depth], NT)
        small = fast_dot(picked_lo[:, 0:depth], matrices[0:64, 0:depth], NT)
        return total + (both[:, 0:64] + both[:, 64:128] + small)

    def far_step(g, total):
        first = pl.multiple_of(g * GROUP, GROUP)
        cube = jnp.swapaxes(far_mats[:, pl.ds(first, GROUP), :], 0, 1)
        return far_block(first, GROUP, cube, total)

    whole = terms // GROUP
    total = lax.fori_loop(0, whole, far_step, jnp.zeros((targets, 64), jnp.float32))
    for t in range(whole * GROUP, terms):
        total = far_block(t, 1, far_mats[:, t, :][None], total)
    far_ref[...] = total[:, 0:terms]


def final_kernel(
    every_top_hbm,
    far_lists_hbm,
    far_mats_hbm,
    far_hbm,
    partial_hbm,
    down_hbm,
    local_hbm,
    out_ref,
    every_top_ref,
    far_lists_ref,
    far_mats_ref,
    far_ref,
    partial_ref,
    down_ref,
    local_ref,
    sems,
    top_lanes,
    sums,
    tops,
    mid,
    low,
):
    blocks = 7
    deep = far_mats_ref.shape[0] // blocks
    pairs = [
        (every_top_hbm, every_top_ref),
        (far_lists_hbm, far_lists_ref),
    ]
    for i in range(blocks):
        part = pl.ds(i * deep, deep)
        pairs.append((far_mats_hbm.at[part], far_mats_ref.at[part]))
    pairs += [
        (far_hbm, far_ref),
        (partial_hbm, partial_ref),
        (down_hbm, down_ref),
        (local_hbm, local_ref),
    ]
    moves = [
        pltpu.make_async_copy(src, dst, sems.at[i]) for i, (src, dst) in enumerate(pairs)
    ]
    for move in moves:
        move.start()
    devices = every_top_ref.shape[0]
    terms = far_ref.shape[1]
    leaves = partial_ref.shape[1]
    mids = leaves // 8
    count = far_lists_ref.shape[0] - leaves - mids
    slots = far_mats_ref.shape[2]
    moves[0].wait()
    moves[1].wait()
    every = every_top_ref[...]
    both = jnp.concatenate([every[:, 0:64], every[:, 64:128]], axis=0)
    tiles = top_lanes.shape[0]
    wide = tiles * LANES
    if wide > both.shape[0]:
        both = jnp.concatenate(
            [both, jnp.zeros((wide - both.shape[0], both.shape[1]), jnp.float32)], axis=0
        )
    for tile in range(tiles):
        top_lanes[tile] = both[tile * LANES : (tile + 1) * LANES].T
    rows = top_lanes.shape[1] // 8
    picked = []
    for j in range(count):
        entry = far_lists_ref[pl.ds(leaves + mids + j, 1), :]
        code = jnp.where(entry < 0, -1, (entry & 1) * devices + (entry >> 1))
        columns = []
        for column in range(0, slots, LANES):
            width = min(LANES, slots - column)
            part = code[:, column : column + width]
            if width < LANES:
                part = jnp.concatenate(
                    [part, jnp.full((1, LANES - width), -1, jnp.int32)], axis=1
                )
            part = jnp.broadcast_to(part, (56, LANES))
            value = jnp.zeros((56, LANES), jnp.float32)
            for tile in range(tiles):
                here = (part >> 7) == tile
                value = jnp.where(
                    here, lane_gather(top_lanes[tile, 0:56, :], part & (LANES - 1)), value
                )
            columns.append(value)
        picked.append(jnp.concatenate(columns, axis=1)[0:terms, 0:slots])

    def top_step(s):
        matrix = far_mats_ref[s]
        for j in range(count):
            sums[j, pl.ds(s, 1), :] = jnp.sum(matrix * picked[j], axis=0, keepdims=True)

    for i in range(blocks):
        moves[2 + i].wait()
        for s in range(i * deep, (i + 1) * deep):
            top_step(s)
    for move in moves[2 + blocks :]:
        move.wait()
    ones = jnp.ones((8, slots), jnp.float32)
    for j in range(count):
        tops[pl.ds(j, 1), :] = exact_dot(ones, sums[j], NT)[0:1]
    top_rows = tops[...]
    for c in range(8):
        matrix = down_ref[pl.ds(c, terms, stride=8), :]
        part = exact_dot(top_rows, matrix, NT)
        mid[pl.ds(c, count, stride=8), :] = part[0:count]
    mid_rows = mid[...] + far_ref[leaves : leaves + mids, :]
    for c in range(8):
        matrix = down_ref[pl.ds(c, terms, stride=8), :]
        low[pl.ds(c, mids, stride=8), :] = exact_dot(mid_rows, matrix, NT)
    low_rows = low[...] + far_ref[0:leaves, :]
    out_ref[...] = partial_ref[...] + exact_dot(local_ref[...].T, low_rows, NT)


def body(
    field,
    contrast,
    incident,
    near_lists,
    far_lists,
    near_mats,
    far_mats,
    up_mats,
    down_mats,
    moment_map,
    local_map,
):
    devices = lax.axis_size(AXES)
    rank = lax.axis_index(AXES)
    cells, leaves = field.shape
    terms = moment_map.shape[0]
    mids = leaves // 8
    slots = far_mats.shape[0]
    assert leaves == LANES and far_lists.shape[1] == 146
    up_rows = up_mats.transpose(1, 0, 2).reshape(8 * terms, terms)
    down_rows = down_mats.transpose(1, 0, 2).reshape(8 * terms, terms)
    far_cube = far_mats.transpose(1, 2, 0)
    far_rows = far_lists.T
    wide = -(-slots // LANES) * LANES
    f32 = jnp.float32

    source, own_tops = pl.pallas_call(
        source_kernel,
        out_shape=(
            jax.ShapeDtypeStruct((cells, leaves), f32),
            jax.ShapeDtypeStruct((devices, LANES), f32),
        ),
        in_specs=[VMEM] * 4,
        out_specs=(VMEM, VMEM),
        scratch_shapes=[pltpu.VMEM((leaves, terms), f32), pltpu.VMEM((mids, terms), f32)],
    )(field, contrast, moment_map, up_rows)

    pairs = [(i, i ^ 1) for i in range(devices)]
    shifted = [(0, 0), (devices - 1, devices - 1)]
    for i in range(1, devices - 1, 2):
        shifted += [(i, i + 1), (i + 1, i)]
    first = lax.ppermute(source, AXES, pairs)
    second = lax.ppermute(source, AXES, shifted)
    every_top = lax.all_to_all(own_tops, AXES, split_axis=0, concat_axis=0, tiled=True)

    odd = jnp.reshape(rank % 2, (1,)).astype(jnp.int32)
    targets = leaves + mids
    near = near_lists.shape[0]
    partial, far_sums = pl.pallas_call(
        local_kernel,
        out_shape=(
            jax.ShapeDtypeStruct((cells, leaves), f32),
            jax.ShapeDtypeStruct((targets, terms), f32),
        ),
        in_specs=[SMEM] + [HBM] * 10,
        out_specs=(VMEM, VMEM),
        scratch_shapes=[
            pltpu.VMEM((cells, leaves), f32),
            pltpu.VMEM((cells, leaves), f32),
            pltpu.VMEM((cells, leaves), f32),
            pltpu.VMEM((cells, leaves), f32),
            pltpu.VMEM((near, leaves), jnp.int32),
            pltpu.VMEM(far_rows.shape, jnp.int32),
            pltpu.VMEM((near, cells, cells), f32),
            pltpu.VMEM((terms, terms, slots), f32),
            pltpu.VMEM((terms, cells), f32),
            pltpu.VMEM((8 * terms, terms), f32),
            pltpu.VMEM((cells, leaves), f32),
            pltpu.VMEM((56, leaves), f32),
            pltpu.VMEM((56, leaves), f32),
            pltpu.VMEM((2 * leaves, terms), f32),
            pltpu.VMEM((2 * mids, terms), f32),
            pltpu.VMEM((56, LANES), f32),
            pltpu.VMEM((targets, wide), jnp.int16),
            pltpu.VMEM((targets, wide), jnp.int16),
            pltpu.VMEM((targets, GROUP * wide), jnp.bfloat16),
            pltpu.VMEM((targets, GROUP * wide), jnp.bfloat16),
            pltpu.VMEM((128, GROUP * wide), jnp.bfloat16),
            pltpu.VMEM((6 * GROUP, 16, LANES), jnp.bfloat16),
            pltpu.SemaphoreType.DMA((10,)),
        ],
    )(
        odd,
        source,
        first,
        second,
        incident,
        near_lists,
        far_rows,
        near_mats,
        far_cube,
        moment_map,
        up_rows,
    )

    tiles = -(-2 * devices // LANES)
    return pl.pallas_call(
        final_kernel,
        out_shape=jax.ShapeDtypeStruct((cells, leaves), f32),
        in_specs=[HBM] * 7,
        out_specs=VMEM,
        scratch_shapes=[
            pltpu.VMEM((devices, LANES), f32),
            pltpu.VMEM(far_rows.shape, jnp.int32),
            pltpu.VMEM((terms, terms, slots), f32),
            pltpu.VMEM((targets, terms), f32),
            pltpu.VMEM((cells, leaves), f32),
            pltpu.VMEM((8 * terms, terms), f32),
            pltpu.VMEM((terms, cells), f32),
            pltpu.SemaphoreType.DMA((13,)),
            pltpu.VMEM((tiles, 64, LANES), f32),
            pltpu.VMEM((2, terms, slots), f32),
            pltpu.VMEM((8, terms), f32),
            pltpu.VMEM((mids, terms), f32),
            pltpu.VMEM((leaves, terms), f32),
        ],
    )(every_top, far_rows, far_cube, far_sums, partial, down_rows, local_map.T)


def solution(mesh):
    columns = P(None, AXES)
    in_specs = (columns,) * 5 + (P(),) * 6
    return jax.shard_map(body, mesh=mesh, in_specs=in_specs, out_specs=columns, check_vma=False)
```

```python
import jax
import jax.numpy as jnp
from jax import lax
from jax.experimental import pallas as pl
from jax.experimental.pallas import tpu as pltpu
from jax.sharding import PartitionSpec as P

AXES = ("group", "owner")
HIGH = lax.Precision.HIGHEST
LANES = 128
GROUP = 8
VMEM = pl.BlockSpec(memory_space=pltpu.VMEM)
SMEM = pl.BlockSpec(memory_space=pltpu.SMEM)
HBM = pl.BlockSpec(memory_space=pltpu.HBM)
NN = (((1,), (0,)), ((), ()))
NT = (((1,), (1,)), ((), ()))
GATHER = lax.GatherDimensionNumbers(
    offset_dims=(),
    collapsed_slice_dims=(1,),
    start_index_map=(1,),
    operand_batching_dims=(0,),
    start_indices_batching_dims=(0,),
)


def lane_gather(values, lanes):
    return lax.gather(
        values,
        lanes[..., None],
        GATHER,
        (1, 1),
        mode=lax.GatherScatterMode.PROMISE_IN_BOUNDS,
    )


def exact_dot(lhs, rhs, dims):
    return lax.dot_general(
        lhs, rhs, dims, precision=HIGH, preferred_element_type=jnp.float32
    )


def fast_dot(lhs, rhs, dims):
    return lax.dot_general(lhs, rhs, dims, preferred_element_type=jnp.float32)


def halves(value):
    upper = value.astype(jnp.bfloat16)
    lower = (value - upper.astype(jnp.float32)).astype(jnp.bfloat16)
    return upper, lower


def split_dot(lhs, rhs, dims):
    (lhs_hi, lhs_lo), (rhs_hi, rhs_lo) = lhs, rhs
    return (
        fast_dot(lhs_hi, rhs_hi, dims)
        + fast_dot(lhs_hi, rhs_lo, dims)
        + fast_dot(lhs_lo, rhs_hi, dims)
    )


def parents_of(children_ref, count, up_ref):
    terms = up_ref.shape[1]
    total = None
    for c in range(8):
        part = exact_dot(
            children_ref[pl.ds(c, count, stride=8), :],
            up_ref[pl.ds(c, terms, stride=8), :],
            NT,
        )
        total = part if total is None else total + part
    return total


def source_kernel(field_ref, contrast_ref, map_ref, up_ref, source_ref, tops_ref, low, mid):
    source = contrast_ref[...] * field_ref[...]
    source_ref[...] = source
    terms = map_ref.shape[0]
    low[...] = exact_dot(map_ref[...], source, NN).T
    mid[...] = parents_of(low, mid.shape[0], up_ref)
    tops = parents_of(mid, mid.shape[0] // 8, up_ref)
    devices = tops_ref.shape[0]
    tops_ref[...] = jnp.zeros(tops_ref.shape, jnp.float32)
    tops_ref[:, 0:terms] = jnp.broadcast_to(tops[0:1], (devices, terms))
    tops_ref[:, 64 : 64 + terms] = jnp.broadcast_to(tops[1:2], (devices, terms))


def levels_of(columns):
    most = jnp.max(jnp.abs(columns), axis=0, keepdims=True)
    some = most > 1e-33
    inverse = jnp.where(some, 32767.0 / jnp.where(some, most, 1.0), 0.0)
    levels = jnp.floor(columns * inverse + 0.5).astype(jnp.int32)
    return levels, most * (1.0 / 32767.0)


def local_kernel(
    odd_ref,
    source_hbm,
    first_hbm,
    second_hbm,
    incident_hbm,
    near_lists_hbm,
    far_lists_hbm,
    near_mats_hbm,
    far_mats_hbm,
    map_hbm,
    up_hbm,
    partial_ref,
    far_ref,
    source_ref,
    first_ref,
    second_ref,
    incident,
    near_lists,
    far_lists,
    near_mats,
    far_mats,
    map_mat,
    up_mat,
    rim,
    low_own,
    low_rim,
    low_rows,
    mid,
    mid_lanes,
    lane_at,
    scale_at,
    picked_a,
    picked_b,
    matrices_a,
    matrices_b,
    spread,
    total,
    steps,
    kind_at,
    sems,
):
    moves = [
        pltpu.make_async_copy(src, dst, sems.at[i])
        for i, (src, dst) in enumerate(
            [
                (map_hbm, map_mat),
                (source_hbm, source_ref),
                (first_hbm, first_ref),
                (second_hbm, second_ref),
                (up_hbm, up_mat),
                (far_lists_hbm, far_lists),
                (near_lists_hbm, near_lists),
                (near_mats_hbm, near_mats),
                (incident_hbm, incident),
                (far_mats_hbm, far_mats),
            ]
        )
    ]
    for move in moves:
        move.start()
    cells, leaves = source_ref.shape
    half = leaves // 2
    terms = map_mat.shape[0]
    mids = leaves // 8
    targets = leaves + mids
    slots = far_mats.shape[2]
    tiles = lane_at.shape[0]
    wide = tiles * LANES
    lane_at[...] = jnp.zeros(lane_at.shape, jnp.int16)
    scale_at[...] = jnp.zeros(scale_at.shape, jnp.float32)
    mid_lanes[...] = jnp.zeros(mid_lanes.shape, jnp.int32)
    lane = lax.broadcasted_iota(jnp.int32, source_ref.shape, 1)
    from_first = (lane // half) == odd_ref[0]
    for move in moves[0:4]:
        move.wait()
    rim[...] = jnp.where(from_first, first_ref[...], second_ref[...])

    own_low = exact_dot(map_mat[...], source_ref[...], NN)
    rim_low = exact_dot(map_mat[...], rim[...], NN)
    own_levels, own_step = levels_of(own_low)
    rim_levels, rim_step = levels_of(rim_low)
    low_own[0:terms, :] = own_levels
    low_rim[0:terms, :] = -rim_levels
    low_rows[0:leaves, :] = own_low.T
    low_rows[leaves : 2 * leaves, :] = rim_low.T
    moves[4].wait()
    mid[...] = parents_of(low_rows, 2 * mids, up_mat)
    mid_levels, mid_step = levels_of(mid[...].T)
    mid_lanes[0:terms, 0 : 2 * mids] = mid_levels
    steps[...] = jnp.zeros(steps.shape, jnp.float32)
    steps[0:1, :] = own_step
    steps[1:2, :] = -rim_step
    steps[2:3, 0 : 2 * mids] = mid_step

    moves[5].wait()
    near_lane = lax.broadcasted_iota(jnp.int32, (8, leaves), 1)
    for i in range(tiles):
        width = min(LANES, slots - i * LANES)
        entry = far_lists[0:targets, i * LANES : i * LANES + width]
        row = lax.broadcasted_iota(jnp.int32, entry.shape, 0)
        leaf = row < leaves
        at = entry + jnp.where(leaf, row - half, row - leaves - mids // 2)
        own = (at >= 0) & (at < jnp.where(leaf, leaves, mids))
        lanes = jnp.where(leaf, at & (leaves - 1), (at & (mids - 1)) + jnp.where(own, 0, mids))
        lane_at[i, :, 0:width] = lanes.astype(jnp.int16)
        kind_at[:, 0:width] = jnp.where(entry < 0, 0, jnp.where(own | (row >= leaves), 1, 2))
        for first in range(0, targets, 8):
            part = slice(first, first + 8)
            at = lane_at[i, part, :].astype(jnp.int32)
            kinds = kind_at[part, :]
            if width < LANES:
                kinds = jnp.where(near_lane < width, kinds, 0)
            if first < leaves:
                own = lane_gather(jnp.broadcast_to(steps[0:1, :], (8, LANES)), at)
                rim_step = lane_gather(jnp.broadcast_to(steps[1:2, :], (8, LANES)), at)
                step = jnp.where(kinds == 1, own, jnp.where(kinds == 2, rim_step, 0.0))
            else:
                step = lane_gather(jnp.broadcast_to(steps[2:3, :], (8, LANES)), at)
                step = jnp.where(kinds == 1, step, 0.0)
            scale_at[i, part, :] = step

    for move in moves[6:9]:
        move.wait()
    def near_step(k, total):
        entry = jnp.broadcast_to(near_lists[pl.ds(k, 1), :], (8, leaves))
        at = near_lane + entry - half
        inside = (at >= 0) & (at < leaves)
        use_own = (entry >= 0) & inside
        use_rim = (entry >= 0) & jnp.logical_not(inside)
        lanes = at & (leaves - 1)
        rows = []
        for r in range(0, cells, 8):
            from_own = lane_gather(source_ref[r : r + 8, :], lanes)
            from_rim = lane_gather(rim[r : r + 8, :], lanes)
            rows.append(
                jnp.where(use_own, from_own, jnp.where(use_rim, from_rim, 0.0))
            )
        picked = halves(jnp.concatenate(rows, axis=0))
        return total + split_dot(halves(near_mats[k]), picked, NN)

    partial_ref[...] = lax.fori_loop(
        0, near_lists.shape[0], near_step, incident[...], unroll=9
    )

    moves[9].wait()
    padding = jnp.zeros((terms, wide - slots), jnp.float32)
    rest = jnp.zeros((64 - terms, wide), jnp.float32)
    total[...] = jnp.zeros(total.shape, jnp.float32)

    def fill(first, count, cube, picked, matrices):
        for u in range(count):
            for i, table in enumerate((low_own, low_rim, mid_lanes)):
                row = jnp.broadcast_to(table[pl.ds(first + u, 1), :], (16, LANES))
                spread[3 * u + i] = row.astype(jnp.int16)
            matrix = jnp.concatenate([cube[u], padding], axis=1)
            matrix = jnp.concatenate([matrix, rest], axis=0)
            upper, lower = halves(matrix)
            for i in range(tiles):
                piece = slice(i * LANES, (i + 1) * LANES)
                matrices[u * tiles + i, 0:64, :] = upper[:, piece]
                matrices[u * tiles + i, 64:128, :] = lower[:, piece]
        for row in range(0, targets, 16):
            for tile in range(tiles):
                lanes = lane_at[tile, row : row + 16, :]
                scale = scale_at[tile, row : row + 16, :]
                use_own = scale > 0.0
                for u in range(count):
                    if row < leaves:
                        value = jnp.where(
                            use_own,
                            lane_gather(spread[3 * u], lanes).astype(jnp.int32),
                            lane_gather(spread[3 * u + 1], lanes).astype(jnp.int32),
                        )
                    else:
                        value = lane_gather(spread[3 * u + 2], lanes).astype(jnp.int32)
                    upper, lower = halves(value.astype(jnp.float32) * scale)
                    picked[u * tiles + tile, row : row + 16, :] = upper
                    picked[u * tiles + tile, targets + row : targets + row + 16, :] = lower

    def add(count, picked, matrices):
        every = range(count * tiles)
        left = jnp.concatenate([picked[i] for i in every], axis=1)
        right = jnp.concatenate([matrices[i] for i in every], axis=1)
        total[...] += fast_dot(left, right, NT)

    def fill_block(g, picked, matrices):
        first = pl.multiple_of(g * GROUP, GROUP)
        cube = jnp.swapaxes(far_mats[:, pl.ds(first, GROUP), :], 0, 1)
        fill(first, GROUP, cube, picked, matrices)

    whole = terms // GROUP
    rounds = (whole - 1) // 2
    fill_block(0, picked_a, matrices_a)

    def two_blocks(i, carry):
        fill_block(2 * i + 1, picked_b, matrices_b)
        add(GROUP, picked_a, matrices_a)
        fill_block(2 * i + 2, picked_a, matrices_a)
        add(GROUP, picked_b, matrices_b)
        return carry

    lax.fori_loop(0, rounds, two_blocks, 0)
    buffers = [(picked_a, matrices_a), (picked_b, matrices_b)]
    for g in range(2 * rounds + 1, whole):
        fill_block(g, *buffers[g % 2])
        add(GROUP, *buffers[(g - 1) % 2])
    add(GROUP, *buffers[(whole - 1) % 2])
    for t in range(whole * GROUP, terms):
        fill(t, 1, far_mats[:, t, :][None], *buffers[whole % 2])
        add(1, *buffers[whole % 2])
    sums = total[0:targets, :] + total[targets : 2 * targets, :]
    far_ref[...] = sums[:, 0:terms] + sums[:, 64 : 64 + terms]


def final_kernel(
    every_top_hbm,
    far_lists_hbm,
    far_mats_hbm,
    far_hbm,
    partial_hbm,
    down_hbm,
    local_hbm,
    out_ref,
    every_top_ref,
    far_lists_ref,
    far_mats_ref,
    far_ref,
    partial_ref,
    down_ref,
    local_ref,
    sems,
    top_lanes,
    sums,
    tops,
    mid,
    low,
):
    blocks = 7
    deep = far_mats_ref.shape[0] // blocks
    pairs = [
        (every_top_hbm, every_top_ref),
        (far_lists_hbm, far_lists_ref),
    ]
    for i in range(blocks):
        part = pl.ds(i * deep, deep)
        pairs.append((far_mats_hbm.at[part], far_mats_ref.at[part]))
    pairs += [
        (far_hbm, far_ref),
        (partial_hbm, partial_ref),
        (down_hbm, down_ref),
        (local_hbm, local_ref),
    ]
    moves = [
        pltpu.make_async_copy(src, dst, sems.at[i]) for i, (src, dst) in enumerate(pairs)
    ]
    for move in moves:
        move.start()
    devices = every_top_ref.shape[0]
    terms = far_ref.shape[1]
    leaves = partial_ref.shape[1]
    mids = leaves // 8
    count = far_lists_ref.shape[0] - leaves - mids
    slots = far_mats_ref.shape[2]
    moves[0].wait()
    moves[1].wait()
    every = every_top_ref[...]
    both = jnp.concatenate([every[:, 0:64], every[:, 64:128]], axis=0)
    tiles = top_lanes.shape[0]
    wide = tiles * LANES
    if wide > both.shape[0]:
        both = jnp.concatenate(
            [both, jnp.zeros((wide - both.shape[0], both.shape[1]), jnp.float32)], axis=0
        )
    for tile in range(tiles):
        top_lanes[tile] = both[tile * LANES : (tile + 1) * LANES].T
    rows = top_lanes.shape[1] // 8
    picked = []
    for j in range(count):
        entry = far_lists_ref[pl.ds(leaves + mids + j, 1), :]
        code = jnp.where(entry < 0, -1, (entry & 1) * devices + (entry >> 1))
        columns = []
        for column in range(0, slots, LANES):
            width = min(LANES, slots - column)
            part = code[:, column : column + width]
            if width < LANES:
                part = jnp.concatenate(
                    [part, jnp.full((1, LANES - width), -1, jnp.int32)], axis=1
                )
            part = jnp.broadcast_to(part, (56, LANES))
            value = jnp.zeros((56, LANES), jnp.float32)
            for tile in range(tiles):
                here = (part >> 7) == tile
                value = jnp.where(
                    here, lane_gather(top_lanes[tile, 0:56, :], part & (LANES - 1)), value
                )
            columns.append(value)
        picked.append(jnp.concatenate(columns, axis=1)[0:terms, 0:slots])

    def top_step(s):
        matrix = far_mats_ref[s]
        for j in range(count):
            sums[j, pl.ds(s, 1), :] = jnp.sum(matrix * picked[j], axis=0, keepdims=True)

    for i in range(blocks):
        moves[2 + i].wait()
        for s in range(i * deep, (i + 1) * deep):
            top_step(s)
    for move in moves[2 + blocks :]:
        move.wait()
    ones = jnp.ones((8, slots), jnp.float32)
    for j in range(count):
        tops[pl.ds(j, 1), :] = exact_dot(ones, sums[j], NT)[0:1]
    top_rows = tops[...]
    for c in range(8):
        matrix = down_ref[pl.ds(c, terms, stride=8), :]
        part = exact_dot(top_rows, matrix, NT)
        mid[pl.ds(c, count, stride=8), :] = part[0:count]
    mid_rows = mid[...] + far_ref[leaves : leaves + mids, :]
    for c in range(8):
        matrix = down_ref[pl.ds(c, terms, stride=8), :]
        low[pl.ds(c, mids, stride=8), :] = exact_dot(mid_rows, matrix, NT)
    low_rows = low[...] + far_ref[0:leaves, :]
    out_ref[...] = partial_ref[...] + exact_dot(local_ref[...].T, low_rows, NT)


def body(
    field,
    contrast,
    incident,
    near_lists,
    far_lists,
    near_mats,
    far_mats,
    up_mats,
    down_mats,
    moment_map,
    local_map,
):
    devices = lax.axis_size(AXES)
    rank = lax.axis_index(AXES)
    cells, leaves = field.shape
    terms = moment_map.shape[0]
    mids = leaves // 8
    slots = far_mats.shape[0]
    assert leaves == LANES and far_lists.shape[1] == 146
    up_rows = up_mats.transpose(1, 0, 2).reshape(8 * terms, terms)
    down_rows = down_mats.transpose(1, 0, 2).reshape(8 * terms, terms)
    far_cube = far_mats.transpose(1, 2, 0)
    far_rows = far_lists.T
    wide = -(-slots // LANES) * LANES
    f32 = jnp.float32

    source, own_tops = pl.pallas_call(
        source_kernel,
        out_shape=(
            jax.ShapeDtypeStruct((cells, leaves), f32),
            jax.ShapeDtypeStruct((devices, LANES), f32),
        ),
        in_specs=[VMEM] * 4,
        out_specs=(VMEM, VMEM),
        scratch_shapes=[pltpu.VMEM((leaves, terms), f32), pltpu.VMEM((mids, terms), f32)],
    )(field, contrast, moment_map, up_rows)

    pairs = [(i, i ^ 1) for i in range(devices)]
    shifted = [(0, 0), (devices - 1, devices - 1)]
    for i in range(1, devices - 1, 2):
        shifted += [(i, i + 1), (i + 1, i)]
    first = lax.ppermute(source, AXES, pairs)
    second = lax.ppermute(source, AXES, shifted)
    every_top = lax.all_to_all(own_tops, AXES, split_axis=0, concat_axis=0, tiled=True)

    odd = jnp.reshape(rank % 2, (1,)).astype(jnp.int32)
    targets = leaves + mids
    near = near_lists.shape[0]
    partial, far_sums = pl.pallas_call(
        local_kernel,
        out_shape=(
            jax.ShapeDtypeStruct((cells, leaves), f32),
            jax.ShapeDtypeStruct((targets, terms), f32),
        ),
        in_specs=[SMEM] + [HBM] * 10,
        out_specs=(VMEM, VMEM),
        scratch_shapes=[
            pltpu.VMEM((cells, leaves), f32),
            pltpu.VMEM((cells, leaves), f32),
            pltpu.VMEM((cells, leaves), f32),
            pltpu.VMEM((cells, leaves), f32),
            pltpu.VMEM((near, leaves), jnp.int32),
            pltpu.VMEM(far_rows.shape, jnp.int32),
            pltpu.VMEM((near, cells, cells), f32),
            pltpu.VMEM((terms, terms, slots), f32),
            pltpu.VMEM((terms, cells), f32),
            pltpu.VMEM((8 * terms, terms), f32),
            pltpu.VMEM((cells, leaves), f32),
            pltpu.VMEM((56, leaves), jnp.int32),
            pltpu.VMEM((56, leaves), jnp.int32),
            pltpu.VMEM((2 * leaves, terms), f32),
            pltpu.VMEM((2 * mids, terms), f32),
            pltpu.VMEM((56, LANES), jnp.int32),
            pltpu.VMEM((wide // LANES, targets, LANES), jnp.int16),
            pltpu.VMEM((wide // LANES, targets, LANES), f32),
            pltpu.VMEM((GROUP * wide // LANES, 2 * targets, LANES), jnp.bfloat16),
            pltpu.VMEM((GROUP * wide // LANES, 2 * targets, LANES), jnp.bfloat16),
            pltpu.VMEM((GROUP * wide // LANES, 128, LANES), jnp.bfloat16),
            pltpu.VMEM((GROUP * wide // LANES, 128, LANES), jnp.bfloat16),
            pltpu.VMEM((3 * GROUP, 16, LANES), jnp.int16),
            pltpu.VMEM((2 * targets, LANES), f32),
            pltpu.VMEM((8, LANES), f32),
            pltpu.VMEM((targets, LANES), jnp.int32),
            pltpu.SemaphoreType.DMA((10,)),
        ],
    )(
        odd,
        source,
        first,
        second,
        incident,
        near_lists,
        far_rows,
        near_mats,
        far_cube,
        moment_map,
        up_rows,
    )

    tiles = -(-2 * devices // LANES)
    return pl.pallas_call(
        final_kernel,
        out_shape=jax.ShapeDtypeStruct((cells, leaves), f32),
        in_specs=[HBM] * 7,
        out_specs=VMEM,
        scratch_shapes=[
            pltpu.VMEM((devices, LANES), f32),
            pltpu.VMEM(far_rows.shape, jnp.int32),
            pltpu.VMEM((terms, terms, slots), f32),
            pltpu.VMEM((targets, terms), f32),
            pltpu.VMEM((cells, leaves), f32),
            pltpu.VMEM((8 * terms, terms), f32),
            pltpu.VMEM((terms, cells), f32),
            pltpu.SemaphoreType.DMA((13,)),
            pltpu.VMEM((tiles, 64, LANES), f32),
            pltpu.VMEM((2, terms, slots), f32),
            pltpu.VMEM((8, terms), f32),
            pltpu.VMEM((mids, terms), f32),
            pltpu.VMEM((leaves, terms), f32),
        ],
    )(every_top, far_rows, far_cube, far_sums, partial, down_rows, local_map.T)


def solution(mesh):
    columns = P(None, AXES)
    in_specs = (columns,) * 5 + (P(),) * 6
    return jax.shard_map(body, mesh=mesh, in_specs=in_specs, out_specs=columns, check_vma=False)
```

```python
import jax
import jax.numpy as jnp
from jax import lax
from jax.experimental import pallas as pl
from jax.experimental.pallas import tpu as pltpu
from jax.sharding import PartitionSpec as P

AXES = ("group", "owner")
LANES = 128
GROUP = 8
VMEM = pl.BlockSpec(memory_space=pltpu.VMEM)
SMEM = pl.BlockSpec(memory_space=pltpu.SMEM)
HBM = pl.BlockSpec(memory_space=pltpu.HBM)
NN = (((1,), (0,)), ((), ()))
NT = (((1,), (1,)), ((), ()))
GATHER = lax.GatherDimensionNumbers(
    offset_dims=(),
    collapsed_slice_dims=(1,),
    start_index_map=(1,),
    operand_batching_dims=(0,),
    start_indices_batching_dims=(0,),
)


def lane_gather(values, lanes):
    return lax.gather(
        values,
        lanes[..., None],
        GATHER,
        (1, 1),
        mode=lax.GatherScatterMode.PROMISE_IN_BOUNDS,
    )


def fast_dot(lhs, rhs, dims):
    return lax.dot_general(lhs, rhs, dims, preferred_element_type=jnp.float32)


def halves(value):
    upper = value.astype(jnp.bfloat16)
    lower = (value - upper.astype(jnp.float32)).astype(jnp.bfloat16)
    return upper, lower


def split_dot(lhs, rhs, dims):
    (lhs_hi, lhs_lo), (rhs_hi, rhs_lo) = lhs, rhs
    return (
        fast_dot(lhs_hi, rhs_hi, dims)
        + fast_dot(lhs_hi, rhs_lo, dims)
        + fast_dot(lhs_lo, rhs_hi, dims)
    )


def parents_of(children_ref, count, up_ref):
    terms = up_ref.shape[1]
    total = None
    for c in range(8):
        part = exact_dot(
            children_ref[pl.ds(c, count, stride=8), :],
            up_ref[pl.ds(c, terms, stride=8), :],
            NT,
        )
        total = part if total is None else total + part
    return total


def exact_dot(lhs, rhs, dims):
    return split_dot(halves(lhs), halves(rhs), dims)


def source_kernel(field_ref, contrast_ref, map_ref, up_ref, source_ref, tops_ref, low, mid):
    source = contrast_ref[...] * field_ref[...]
    source_ref[...] = source
    terms = map_ref.shape[0]
    low[...] = exact_dot(map_ref[...], source, NN).T
    mid[...] = parents_of(low, mid.shape[0], up_ref)
    tops = parents_of(mid, mid.shape[0] // 8, up_ref)
    devices = tops_ref.shape[0]
    tops_ref[...] = jnp.zeros(tops_ref.shape, jnp.float32)
    tops_ref[:, 0:terms] = jnp.broadcast_to(tops[0:1], (devices, terms))
    tops_ref[:, 64 : 64 + terms] = jnp.broadcast_to(tops[1:2], (devices, terms))


def levels_of(columns):
    most = jnp.max(jnp.abs(columns), axis=0, keepdims=True)
    some = most > 1e-33
    inverse = jnp.where(some, 32767.0 / jnp.where(some, most, 1.0), 0.0)
    levels = jnp.floor(columns * inverse + 0.5).astype(jnp.int32)
    return levels, most * (1.0 / 32767.0)


def local_kernel(
    odd_ref,
    source_hbm,
    first_hbm,
    second_hbm,
    incident_hbm,
    near_lists_hbm,
    far_lists_hbm,
    near_mats_hbm,
    far_mats_hbm,
    map_hbm,
    up_hbm,
    partial_ref,
    far_ref,
    source_ref,
    first_ref,
    second_ref,
    incident,
    near_lists,
    far_lists,
    near_mats,
    far_mats,
    map_mat,
    up_mat,
    rim,
    low_own,
    low_rim,
    low_rows,
    mid,
    mid_lanes,
    lane_at,
    scale_at,
    picked_a,
    picked_b,
    matrices_a,
    matrices_b,
    picked_c,
    matrices_c,
    spread,
    total,
    steps,
    kind_at,
    sems,
):
    moves = [
        pltpu.make_async_copy(src, dst, sems.at[i])
        for i, (src, dst) in enumerate(
            [
                (map_hbm, map_mat),
                (source_hbm, source_ref),
                (first_hbm, first_ref),
                (second_hbm, second_ref),
                (up_hbm, up_mat),
                (far_lists_hbm, far_lists),
                (near_lists_hbm, near_lists),
                (near_mats_hbm, near_mats),
                (incident_hbm, incident),
                (far_mats_hbm, far_mats),
            ]
        )
    ]
    for move in moves:
        move.start()
    cells, leaves = source_ref.shape
    half = leaves // 2
    terms = map_mat.shape[0]
    mids = leaves // 8
    targets = leaves + mids
    slots = far_mats.shape[2]
    tiles = lane_at.shape[0]
    wide = tiles * LANES
    lane_at[...] = jnp.zeros(lane_at.shape, jnp.int16)
    scale_at[...] = jnp.zeros(scale_at.shape, jnp.float32)
    mid_lanes[...] = jnp.zeros(mid_lanes.shape, jnp.int32)
    lane = lax.broadcasted_iota(jnp.int32, source_ref.shape, 1)
    from_first = (lane // half) == odd_ref[0]
    for move in moves[0:9]:
        move.wait()
    rim[...] = jnp.where(from_first, first_ref[...], second_ref[...])

    own_low = exact_dot(map_mat[...], source_ref[...], NN)
    rim_low = exact_dot(map_mat[...], rim[...], NN)
    own_levels, own_step = levels_of(own_low)
    rim_levels, rim_step = levels_of(rim_low)
    low_own[0:terms, :] = own_levels
    low_rim[0:terms, :] = -rim_levels
    low_rows[0:leaves, :] = own_low.T
    low_rows[leaves : 2 * leaves, :] = rim_low.T
    mid[...] = parents_of(low_rows, 2 * mids, up_mat)
    mid_levels, mid_step = levels_of(mid[...].T)
    mid_lanes[0:terms, 0 : 2 * mids] = mid_levels
    steps[...] = jnp.zeros(steps.shape, jnp.float32)
    steps[0:1, :] = own_step
    steps[1:2, :] = -rim_step
    steps[2:3, 0 : 2 * mids] = mid_step

    near_lane = lax.broadcasted_iota(jnp.int32, (8, leaves), 1)
    for i in range(tiles):
        width = min(LANES, slots - i * LANES)
        entry = far_lists[0:targets, i * LANES : i * LANES + width]
        row = lax.broadcasted_iota(jnp.int32, entry.shape, 0)
        leaf = row < leaves
        at = entry + jnp.where(leaf, row - half, row - leaves - mids // 2)
        own = (at >= 0) & (at < jnp.where(leaf, leaves, mids))
        lanes = jnp.where(leaf, at & (leaves - 1), (at & (mids - 1)) + jnp.where(own, 0, mids))
        lane_at[i, :, 0:width] = lanes.astype(jnp.int16)
        kind_at[:, 0:width] = jnp.where(entry < 0, 0, jnp.where(own | (row >= leaves), 1, 2))
        for first in range(0, targets, 8):
            part = slice(first, first + 8)
            at = lane_at[i, part, :].astype(jnp.int32)
            kinds = kind_at[part, :]
            if width < LANES:
                kinds = jnp.where(near_lane < width, kinds, 0)
            if first < leaves:
                own = lane_gather(jnp.broadcast_to(steps[0:1, :], (8, LANES)), at)
                rim_step = lane_gather(jnp.broadcast_to(steps[1:2, :], (8, LANES)), at)
                step = jnp.where(kinds == 1, own, jnp.where(kinds == 2, rim_step, 0.0))
            else:
                step = lane_gather(jnp.broadcast_to(steps[2:3, :], (8, LANES)), at)
                step = jnp.where(kinds == 1, step, 0.0)
            scale_at[i, part, :] = step

    def near_step(k, total):
        entry = jnp.broadcast_to(near_lists[pl.ds(k, 1), :], (8, leaves))
        at = near_lane + entry - half
        inside = (at >= 0) & (at < leaves)
        use_own = (entry >= 0) & inside
        use_rim = (entry >= 0) & jnp.logical_not(inside)
        lanes = at & (leaves - 1)
        rows = []
        for r in range(0, cells, 8):
            from_own = lane_gather(source_ref[r : r + 8, :], lanes)
            from_rim = lane_gather(rim[r : r + 8, :], lanes)
            rows.append(
                jnp.where(use_own, from_own, jnp.where(use_rim, from_rim, 0.0))
            )
        picked = halves(jnp.concatenate(rows, axis=0))
        return total + split_dot(halves(near_mats[k]), picked, NN)

    near = incident[...]
    for k in range(near_lists.shape[0]):
        near = near_step(k, near)
    partial_ref[...] = near

    moves[9].wait()
    padding = jnp.zeros((terms, wide - slots), jnp.float32)
    rest = jnp.zeros((64 - terms, wide), jnp.float32)
    total[...] = jnp.zeros(total.shape, jnp.float32)

    def fill(first, count, cube, picked, matrices):
        for u in range(count):
            for i, table in enumerate((low_own, low_rim, mid_lanes)):
                row = jnp.broadcast_to(table[pl.ds(first + u, 1), :], (16, LANES))
                spread[3 * u + i] = row.astype(jnp.int16)
            matrix = jnp.concatenate([cube[u], padding], axis=1)
            matrix = jnp.concatenate([matrix, rest], axis=0)
            upper, lower = halves(matrix)
            for i in range(tiles):
                piece = slice(i * LANES, (i + 1) * LANES)
                matrices[u * tiles + i, 0:64, :] = upper[:, piece]
                matrices[u * tiles + i, 64:128, :] = lower[:, piece]
        for row in range(0, targets, 16):
            for tile in range(tiles):
                lanes = lane_at[tile, row : row + 16, :]
                scale = scale_at[tile, row : row + 16, :]
                use_own = scale > 0.0
                for u in range(count):
                    if row < leaves:
                        value = jnp.where(
                            use_own,
                            lane_gather(spread[3 * u], lanes).astype(jnp.int32),
                            lane_gather(spread[3 * u + 1], lanes).astype(jnp.int32),
                        )
                    else:
                        value = lane_gather(spread[3 * u + 2], lanes).astype(jnp.int32)
                    upper, lower = halves(value.astype(jnp.float32) * scale)
                    picked[u * tiles + tile, row : row + 16, :] = upper
                    picked[u * tiles + tile, targets + row : targets + row + 16, :] = lower

    def add(count, picked, matrices):
        every = range(count * tiles)
        left = jnp.concatenate([picked[i] for i in every], axis=1)
        right = jnp.concatenate([matrices[i] for i in every], axis=1)
        total[...] += fast_dot(left, right, NT)

    def fill_block(g, picked, matrices):
        first = pl.multiple_of(g * GROUP, GROUP)
        cube = jnp.swapaxes(far_mats[:, pl.ds(first, GROUP), :], 0, 1)
        fill(first, GROUP, cube, picked, matrices)

    whole = terms // GROUP
    rounds = (whole - 1) // 2
    fill_block(0, picked_a, matrices_a)
    for t in range(whole * GROUP, terms):
        fill(t, 1, far_mats[:, t, :][None], picked_c, matrices_c)
        add(1, picked_c, matrices_c)

    def two_blocks(i, carry):
        fill_block(2 * i + 1, picked_b, matrices_b)
        add(GROUP, picked_a, matrices_a)
        fill_block(2 * i + 2, picked_a, matrices_a)
        add(GROUP, picked_b, matrices_b)
        return carry

    lax.fori_loop(0, rounds, two_blocks, 0)
    buffers = [(picked_a, matrices_a), (picked_b, matrices_b)]
    for g in range(2 * rounds + 1, whole):
        fill_block(g, *buffers[g % 2])
        add(GROUP, *buffers[(g - 1) % 2])
    add(GROUP, *buffers[(whole - 1) % 2])
    sums = total[0:targets, :] + total[targets : 2 * targets, :]
    far_ref[...] = sums[:, 0:terms] + sums[:, 64 : 64 + terms]


def final_kernel(
    every_top_hbm,
    far_lists_hbm,
    far_mats_hbm,
    far_hbm,
    partial_hbm,
    down_hbm,
    local_hbm,
    out_ref,
    every_top_ref,
    far_lists_ref,
    far_mats_ref,
    far_ref,
    partial_ref,
    down_ref,
    local_ref,
    sems,
    top_lanes,
    sums,
    tops,
    mid,
    low,
):
    blocks = 7
    deep = far_mats_ref.shape[0] // blocks
    pairs = [
        (every_top_hbm, every_top_ref),
        (far_lists_hbm, far_lists_ref),
    ]
    for i in range(blocks):
        part = pl.ds(i * deep, deep)
        pairs.append((far_mats_hbm.at[part], far_mats_ref.at[part]))
    pairs += [
        (far_hbm, far_ref),
        (partial_hbm, partial_ref),
        (down_hbm, down_ref),
        (local_hbm, local_ref),
    ]
    moves = [
        pltpu.make_async_copy(src, dst, sems.at[i]) for i, (src, dst) in enumerate(pairs)
    ]
    for move in moves:
        move.start()
    devices = every_top_ref.shape[0]
    terms = far_ref.shape[1]
    leaves = partial_ref.shape[1]
    mids = leaves // 8
    count = far_lists_ref.shape[0] - leaves - mids
    slots = far_mats_ref.shape[2]
    moves[0].wait()
    moves[1].wait()
    every = every_top_ref[...]
    both = jnp.concatenate([every[:, 0:64], every[:, 64:128]], axis=0)
    tiles = top_lanes.shape[0]
    wide = tiles * LANES
    if wide > both.shape[0]:
        both = jnp.concatenate(
            [both, jnp.zeros((wide - both.shape[0], both.shape[1]), jnp.float32)], axis=0
        )
    for tile in range(tiles):
        top_lanes[tile] = both[tile * LANES : (tile + 1) * LANES].T
    rows = top_lanes.shape[1] // 8
    picked = []
    for j in range(count):
        entry = far_lists_ref[pl.ds(leaves + mids + j, 1), :]
        code = jnp.where(entry < 0, -1, (entry & 1) * devices + (entry >> 1))
        columns = []
        for column in range(0, slots, LANES):
            width = min(LANES, slots - column)
            part = code[:, column : column + width]
            if width < LANES:
                part = jnp.concatenate(
                    [part, jnp.full((1, LANES - width), -1, jnp.int32)], axis=1
                )
            part = jnp.broadcast_to(part, (56, LANES))
            value = jnp.zeros((56, LANES), jnp.float32)
            for tile in range(tiles):
                here = (part >> 7) == tile
                value = jnp.where(
                    here, lane_gather(top_lanes[tile, 0:56, :], part & (LANES - 1)), value
                )
            columns.append(value)
        picked.append(jnp.concatenate(columns, axis=1)[0:terms, 0:slots])

    for i in range(blocks):
        moves[2 + i].wait()
        for s in range(i * deep, (i + 1) * deep):
            matrix = far_mats_ref[s]
            for j in range(count):
                sums[j, s : s + 1, :] = jnp.sum(matrix * picked[j], axis=0, keepdims=True)
    for move in moves[2 + blocks :]:
        move.wait()
    ones = jnp.ones((8, slots), jnp.float32)
    tops[...] = jnp.zeros(tops.shape, jnp.float32)
    for j in range(count):
        tops[pl.ds(j, 1), :] = exact_dot(ones, sums[j], NT)[0:1]
    top_rows = tops[...]
    for c in range(8):
        matrix = down_ref[pl.ds(c, terms, stride=8), :]
        part = exact_dot(top_rows, matrix, NT)
        mid[pl.ds(c, count, stride=8), :] = part[0:count]
    mid_rows = mid[...] + far_ref[leaves : leaves + mids, :]
    for c in range(8):
        matrix = down_ref[pl.ds(c, terms, stride=8), :]
        low[pl.ds(c, mids, stride=8), :] = exact_dot(mid_rows, matrix, NT)
    low_rows = low[...] + far_ref[0:leaves, :]
    out_ref[...] = partial_ref[...] + exact_dot(local_ref[...].T, low_rows, NT)


def body(
    field,
    contrast,
    incident,
    near_lists,
    far_lists,
    near_mats,
    far_mats,
    up_mats,
    down_mats,
    moment_map,
    local_map,
):
    devices = lax.axis_size(AXES)
    rank = lax.axis_index(AXES)
    cells, leaves = field.shape
    terms = moment_map.shape[0]
    mids = leaves // 8
    slots = far_mats.shape[0]
    assert leaves == LANES and far_lists.shape[1] == 146
    up_rows = up_mats.transpose(1, 0, 2).reshape(8 * terms, terms)
    down_rows = down_mats.transpose(1, 0, 2).reshape(8 * terms, terms)
    far_cube = far_mats.transpose(1, 2, 0)
    far_rows = far_lists.T
    wide = -(-slots // LANES) * LANES
    f32 = jnp.float32

    source, own_tops = pl.pallas_call(
        source_kernel,
        out_shape=(
            jax.ShapeDtypeStruct((cells, leaves), f32),
            jax.ShapeDtypeStruct((devices, LANES), f32),
        ),
        in_specs=[VMEM] * 4,
        out_specs=(VMEM, VMEM),
        scratch_shapes=[pltpu.VMEM((leaves, terms), f32), pltpu.VMEM((mids, terms), f32)],
    )(field, contrast, moment_map, up_rows)

    pairs = [(i, i ^ 1) for i in range(devices)]
    shifted = [(0, 0), (devices - 1, devices - 1)]
    for i in range(1, devices - 1, 2):
        shifted += [(i, i + 1), (i + 1, i)]
    first = lax.ppermute(source, AXES, pairs)
    second = lax.ppermute(source, AXES, shifted)
    every_top = lax.all_to_all(own_tops, AXES, split_axis=0, concat_axis=0, tiled=True)

    odd = jnp.reshape(rank % 2, (1,)).astype(jnp.int32)
    targets = leaves + mids
    near = near_lists.shape[0]
    partial, far_sums = pl.pallas_call(
        local_kernel,
        out_shape=(
            jax.ShapeDtypeStruct((cells, leaves), f32),
            jax.ShapeDtypeStruct((targets, terms), f32),
        ),
        in_specs=[SMEM] + [HBM] * 10,
        out_specs=(VMEM, VMEM),
        scratch_shapes=[
            pltpu.VMEM((cells, leaves), f32),
            pltpu.VMEM((cells, leaves), f32),
            pltpu.VMEM((cells, leaves), f32),
            pltpu.VMEM((cells, leaves), f32),
            pltpu.VMEM((near, leaves), jnp.int32),
            pltpu.VMEM(far_rows.shape, jnp.int32),
            pltpu.VMEM((near, cells, cells), f32),
            pltpu.VMEM((terms, terms, slots), f32),
            pltpu.VMEM((terms, cells), f32),
            pltpu.VMEM((8 * terms, terms), f32),
            pltpu.VMEM((cells, leaves), f32),
            pltpu.VMEM((56, leaves), jnp.int32),
            pltpu.VMEM((56, leaves), jnp.int32),
            pltpu.VMEM((2 * leaves, terms), f32),
            pltpu.VMEM((2 * mids, terms), f32),
            pltpu.VMEM((56, LANES), jnp.int32),
            pltpu.VMEM((wide // LANES, targets, LANES), jnp.int16),
            pltpu.VMEM((wide // LANES, targets, LANES), f32),
            pltpu.VMEM((GROUP * wide // LANES, 2 * targets, LANES), jnp.bfloat16),
            pltpu.VMEM((GROUP * wide // LANES, 2 * targets, LANES), jnp.bfloat16),
            pltpu.VMEM((GROUP * wide // LANES, 128, LANES), jnp.bfloat16),
            pltpu.VMEM((GROUP * wide // LANES, 128, LANES), jnp.bfloat16),
            pltpu.VMEM((wide // LANES, 2 * targets, LANES), jnp.bfloat16),
            pltpu.VMEM((wide // LANES, 128, LANES), jnp.bfloat16),
            pltpu.VMEM((3 * GROUP, 16, LANES), jnp.int16),
            pltpu.VMEM((2 * targets, LANES), f32),
            pltpu.VMEM((8, LANES), f32),
            pltpu.VMEM((targets, LANES), jnp.int32),
            pltpu.SemaphoreType.DMA((10,)),
        ],
    )(
        odd,
        source,
        first,
        second,
        incident,
        near_lists,
        far_rows,
        near_mats,
        far_cube,
        moment_map,
        up_rows,
    )

    tiles = -(-2 * devices // LANES)
    return pl.pallas_call(
        final_kernel,
        out_shape=jax.ShapeDtypeStruct((cells, leaves), f32),
        in_specs=[HBM] * 7,
        out_specs=VMEM,
        scratch_shapes=[
            pltpu.VMEM((devices, LANES), f32),
            pltpu.VMEM(far_rows.shape, jnp.int32),
            pltpu.VMEM((terms, terms, slots), f32),
            pltpu.VMEM((targets, terms), f32),
            pltpu.VMEM((cells, leaves), f32),
            pltpu.VMEM((8 * terms, terms), f32),
            pltpu.VMEM((terms, cells), f32),
            pltpu.SemaphoreType.DMA((13,)),
            pltpu.VMEM((tiles, 64, LANES), f32),
            pltpu.VMEM((2, terms, slots), f32),
            pltpu.VMEM((8, terms), f32),
            pltpu.VMEM((mids, terms), f32),
            pltpu.VMEM((leaves, terms), f32),
        ],
        compiler_params=pltpu.CompilerParams(vmem_limit_bytes=55200 << 10),
    )(every_top, far_rows, far_cube, far_sums, partial, down_rows, local_map.T)


def solution(mesh):
    columns = P(None, AXES)
    in_specs = (columns,) * 5 + (P(),) * 6
    return jax.shard_map(body, mesh=mesh, in_specs=in_specs, out_specs=columns, check_vma=False)
```
